32 devices in a mesh: arc: 4 (over x, core), par: 8 (over z, y).
Axes of the slice: x: 2, y: 2, z: 4, core: 2. Of those that a mesh axis runs over, the one named last changes fastest.
Arguments:
- observations: float32 [1024, 32768], P('arc', 'par'), may hold values from -18 to 18
- arc_mask: int32 [8, 256], P('arc', 'par'), may hold values 0 or 1
- panel_owner: int32 [2], replicated, may hold values from 0 to 127, as said below
Outputs:
- info_rows: float32 [512, 32768], P('arc', 'par')
The draws below stay inside these ranges and needn't reach their ends.
Inputs may be any that keep to these rules, and one draw needn't show every extreme that they name: `panel_owner`: two different panel indices below 128; one of the two is always the last panel.
All inputs are finite; a program needn't handle non-finite values. No bound on the sum of `arc_mask` on one device may be relied on, other than what follows from the above.
Results may differ from the reference program's by a relative error of at most 0.002.
Values sent between devices are 32-bit elements; how exact they have to be, the bound alone decides.
No kernel may reach another device: no remote copies, remote signals or barrier semaphores. Data moves between devices by JAX's collectives and lax.ppermute only.
A program may use at most 64 MiB of HBM per device.

```python
import math
import jax
import jax.numpy as jnp
from jax import lax

PANEL = 256
BLK = 128
ROWS = 1024
COLS = 32768


def draw_observations(key, part):
    row_key = jax.random.fold_in(key, 21)
    value_key = jax.random.fold_in(key, 23)
    common_key = jax.random.fold_in(key, 24)
    twin_key = jax.random.fold_in(key, 25)
    row_scale = jnp.exp(jax.random.uniform(row_key, (ROWS, 1), jnp.float32, math.log(0.3), math.log(3.0)))
    common = jnp.clip(jax.random.normal(common_key, (ROWS, 1), jnp.float32), -6.0, 6.0)
    twin_noise = jnp.clip(jax.random.normal(twin_key, (ROWS, 1), jnp.float32), -6.0, 6.0)
    values = jnp.clip(jax.random.normal(value_key, (ROWS, COLS), jnp.float32), -6.0, 6.0)
    share = 0.1
    base = math.sqrt(1.0 - share) * values + math.sqrt(share) * common
    twin_col = base[:, COLS - 2:COLS - 1] + 0.015 * twin_noise
    joined = jnp.concatenate([base[:, :COLS - 1], twin_col], 1)
    scaled = joined * row_scale
    return jnp.clip(scaled, -18.0, 18.0).astype(jnp.float32)


def draw_panel_owner(key, part):
    last_panel = COLS // PANEL - 1
    other_panel = jax.random.randint(jax.random.fold_in(key, 31), (), 0, last_panel)
    order_bit = jax.random.randint(jax.random.fold_in(key, 32), (), 0, 2)
    first_index = jnp.where(order_bit == 0, other_panel, last_panel)
    second_index = jnp.where(order_bit == 0, last_panel, other_panel)
    return jnp.stack([first_index, second_index]).astype(jnp.int32)


def set_ends(array, own_key, smallest, top_value):
    longest = array.shape.index(max(array.shape))
    spots = []
    for shift in (0, 1):
        where = [jax.random.randint(jax.random.fold_in(own_key, axis), (), 0, length) for axis, length in enumerate(array.shape)]
        where[longest] = (where[longest] + shift) % array.shape[longest]
        spots.append(tuple(where))
    return array.at[spots[0]].set(smallest).at[spots[1]].set(top_value)


def setup_inputs(seed: int = 0) -> dict:
    seeds = jax.random.split(jax.random.key(seed), 4)
    observations = draw_observations(jax.random.fold_in(seeds[3], 71), 0)
    arc_mask = set_ends((jax.random.randint(seeds[1], (ROWS // BLK, COLS // BLK), 0, 4) < 3).astype(jnp.int32), jax.random.fold_in(seeds[1], 1), 0, 1)
    panel_owner = draw_panel_owner(jax.random.fold_in(seeds[3], 71), 0)
    return {"observations": observations, "arc_mask": arc_mask, "panel_owner": panel_owner}


def inner_high(left, right):
    return lax.dot_general(left, right, (((0,), (0,)), ((), ())), precision=lax.Precision.HIGHEST, preferred_element_type=left.dtype)

def matmul_high(left, right):
    return jnp.dot(left, right, precision=lax.Precision.HIGHEST, preferred_element_type=left.dtype)

def expand_mask(observations, arc_mask):
    row_blocks, col_blocks = arc_mask.shape
    shaped = observations.reshape(row_blocks, BLK, col_blocks, BLK)
    masked = shaped * arc_mask.astype(observations.dtype)[:, None, :, None]
    return masked.reshape(observations.shape) / math.sqrt(ROWS)

def reference(observations, arc_mask, panel_owner):
    design = expand_mask(observations, arc_mask)
    rows_out = []
    for panel_turn in range(2):
        col_start = (panel_owner[panel_turn] * PANEL).astype(jnp.int32)
        panel_cols = lax.dynamic_slice_in_dim(design, col_start, PANEL, 1)
        gram_block = inner_high(panel_cols, panel_cols)
        cross_sums = inner_high(panel_cols, design)
        chol_lower = jnp.linalg.cholesky(gram_block)
        factor = jax.scipy.linalg.solve_triangular(chol_lower, cross_sums, lower=True)
        rows_out.append(factor)
        if panel_turn == 0:
            coefficients = jax.scipy.linalg.solve_triangular(chol_lower.T, factor, lower=False)
            design = design - matmul_high(panel_cols, coefficients)
    return jnp.concatenate(rows_out, 0)
```

```python
import functools

import jax
import jax.numpy as jnp
from jax import lax
from jax.experimental import pallas as pl
from jax.experimental.pallas import tpu as pltpu
from jax.sharding import PartitionSpec as P

PANEL = 256
BLK = 128
CORES = 2
CHUNKS = 4
HI = lax.Precision.HIGHEST
SUB, LANE = 8, 128

def full(row):
    return jnp.broadcast_to(row, (SUB, LANE))

def small_factor(diag):
    a = dict(diag)
    l, inv = {}, {}
    for j in range(SUB):
        inv[j] = lax.rsqrt(a[j, j])
        for i in range(j + 1, SUB):
            l[i, j] = a[i, j] * inv[j]
        for i in range(j + 1, SUB):
            for m in range(j + 1, i + 1):
                a[i, m] = a[i, m] - l[i, j] * l[m, j]
    t = {}
    for j in range(SUB):
        t[j, j] = inv[j]
        for i in range(j + 1, SUB):
            acc = l[i, j] * t[j, j]
            for m in range(j + 1, i):
                acc = acc + l[i, m] * t[m, j]
            t[i, j] = -(acc * inv[i])
    return t

def factor_block(tiles, offset):
    count = len(tiles)
    lanes = lax.broadcasted_iota(jnp.int32, (SUB, LANE), 1)
    subs = lax.broadcasted_iota(jnp.int32, (SUB, LANE), 0)
    tiles = list(tiles)
    for s in range(count):
        base = offset + s * SUB
        cols = {}
        for i in range(s, count):
            for c in range(SUB):
                cols[i, c] = jnp.broadcast_to(tiles[i][:, base + c:base + c + 1], (SUB, LANE))
        diag = {(i, j): full(cols[s, j][i:i + 1, :]) for i in range(SUB) for j in range(i + 1)}
        t = small_factor(diag)
        in_diag = (lanes >= base) & (lanes < base + SUB)
        unit = jnp.where(lanes == base + subs, 1.0, 0.0)
        own = jnp.where(in_diag, unit, tiles[s])
        rows = [full(own[c:c + 1, :]) for c in range(SUB)]
        new = []
        for c in range(SUB):
            acc = t[c, 0] * rows[0]
            for m in range(1, c + 1):
                acc = acc + t[c, m] * rows[m]
            new.append(acc)
        merged = new[0]
        for c in range(1, SUB):
            merged = jnp.where(subs == c, new[c], merged)
        tiles[s] = merged
        for i in range(s + 1, count):
            step = None
            for c in range(SUB):
                mult = t[c, 0] * cols[i, 0]
                for m in range(1, c + 1):
                    mult = mult + t[c, m] * cols[i, m]
                step = mult * new[c] if step is None else step + mult * new[c]
            tiles[i] = jnp.where(in_diag, 0.0, tiles[i]) - step
    return tiles

def nt(a, b):
    return lax.dot_general(a, b, (((1,), (1,)), ((), ())), precision=HI, preferred_element_type=jnp.float32)

def nn(a, b):
    return jnp.dot(a, b, precision=HI, preferred_element_type=jnp.float32)

def chol_inv_kernel(nb, g_ref, x_ref):
    n = g_ref.shape[0]
    for j in range(0, n, LANE):
        x_ref[j:n, j:j + LANE] = g_ref[j:n, j:j + LANE]
        if j:
            x_ref[0:j, j:j + LANE] = jnp.zeros((j, LANE), jnp.float32)
    for k in range(n // nb):
        lo, hi = k * nb, (k + 1) * nb
        lane0 = lo // LANE * LANE
        off = lo - lane0
        tiles = [x_ref[lo + SUB * i: lo + SUB * (i + 1), lane0:lane0 + LANE] for i in range(nb // SUB)]
        done = factor_block(tiles, off)
        rows = lax.broadcasted_iota(jnp.int32, (nb, LANE), 0)
        lanes = lax.broadcasted_iota(jnp.int32, (nb, LANE), 1)
        block = jnp.concatenate(done, 0)
        keep = lanes <= rows + off
        inv_rows = jnp.where(keep, block, 0.0)
        t_wide = jnp.where(lanes >= off, inv_rows, 0.0)
        t_sq = t_wide[:, off:off + nb]
        if lane0:
            left = nn(t_sq, x_ref[lo:hi, 0:lane0])
            x_ref[lo:hi, 0:lane0] = left
        x_ref[lo:hi, lane0:lane0 + LANE] = inv_rows
        if hi < n:
            low = nt(x_ref[hi:n, lane0:lane0 + LANE], t_wide)
            rl = lax.broadcasted_iota(jnp.int32, (n - hi, LANE), 1)
            x_ref[hi:n, lane0:lane0 + LANE] = jnp.where((rl >= off) & (rl < off + nb), 0.0, x_ref[hi:n, lane0:lane0 + LANE])
            x_ref[hi:n, 0:lane0 + LANE] -= nn(low, x_ref[lo:hi, 0:lane0 + LANE])
            for c in range(hi // LANE * LANE, n, LANE):
                c0 = max(c, hi)
                x_ref[c0:n, c0:c + LANE] -= nt(low[c0 - hi:], low[c0 - hi:c + LANE - hi])
    return


def chol_inv(gram):
    n = gram.shape[0]
    return pl.pallas_call(
        functools.partial(chol_inv_kernel, 64),
        out_shape=jax.ShapeDtypeStruct((n, n), jnp.float32),
        in_specs=[pl.BlockSpec(memory_space=pltpu.VMEM)],
        out_specs=pl.BlockSpec(memory_space=pltpu.VMEM),
        cost_estimate=pl.CostEstimate(flops=2 * n * n * n, bytes_accessed=8 * n * n, transcendentals=n),
        name="chol_inv",
    )(gram)


def shift(array, axis, step):
    size = lax.axis_size(axis)
    return lax.ppermute(array, axis, [(i, (i + step) % size) for i in range(size)])


def swap_core(array):
    return lax.ppermute(array, "arc", [(i, i ^ 1) for i in range(lax.axis_size("arc"))])


def spread_panels(free_cols, free_root, last_cols):
    count, here = lax.axis_size("par"), lax.axis_index("par")
    rows = free_cols.shape[0]
    part = rows // count
    pieces = free_cols.reshape(count, part, PANEL)
    last_pieces = last_cols.reshape(count, part, PANEL)
    free_mine = lax.dynamic_index_in_dim(pieces, here, 0, keepdims=False)
    last_mine = last_pieces[count - 1]
    for step in range(1, count):
        target = (here + step) % count
        got = shift(lax.dynamic_index_in_dim(pieces, target, 0, keepdims=False), "par", step)
        free_mine = jnp.where((here + count - step) % count == free_root, got, free_mine)
        dest = step - 1
        sent = lax.ppermute(last_pieces[dest], "par", [(count - 1, dest)])
        last_mine = jnp.where(here == dest, sent, last_mine)
    mine = jnp.concatenate([free_mine, last_mine], 1)
    stack = [mine] + [shift(mine, "par", step) for step in range(1, count)]
    turned = jnp.stack(stack[::-1] + stack[::-1], 0)
    return lax.dynamic_slice_in_dim(turned, count - 1 - here, count, 0).reshape(rows, 2 * PANEL)


def shards(observations, arc_mask, panel_owner):
    row_count, col_count = observations.shape
    arcs, pars = lax.axis_size("arc"), lax.axis_size("par")
    chips = arcs // CORES
    core = lax.axis_index("arc") % CORES
    chip = lax.axis_index("arc") // CORES
    scale = 1.0 / (row_count * arcs) ** 0.5
    local_panels = col_count // PANEL
    last_panel = pars * local_panels - 1
    last_first = panel_owner[0] == last_panel
    free = jnp.where(last_first, panel_owner[1], panel_owner[0])
    row_blocks, col_blocks = arc_mask.shape

    def masked(cols, marks):
        shaped = cols.reshape(row_blocks, BLK, marks.shape[1], BLK)
        return (shaped * (marks.astype(jnp.float32) * scale)[:, None, :, None]).reshape(cols.shape)

    def window(start, size):
        cols = lax.dynamic_slice_in_dim(observations, start, size, 1)
        marks = lax.dynamic_slice_in_dim(arc_mask, start // BLK, size // BLK, 1)
        return masked(cols, marks)

    free_cols = window((free % local_panels) * PANEL, PANEL)
    last_cols = masked(observations[:, -PANEL:], arc_mask[:, -PANEL // BLK:])
    panels = spread_panels(free_cols, free // local_panels, last_cols)
    left, right = panels[:, :PANEL], panels[:, PANEL:]
    panels = jnp.concatenate([jnp.where(last_first, right, left), jnp.where(last_first, left, right)], 1)

    half = col_count // CORES
    keep = window(core * half, half)
    give = window((1 - core) * half, half)
    own = jnp.stack([keep, swap_core(give)], 0)

    near = [panels] + [shift(panels, "arc", CORES * step) for step in range(1, chips)]
    far = swap_core(jnp.stack(near, 0))
    tall = jnp.concatenate([block for step in range(chips) for block in (near[step], far[step])], 0)

    inverse = chol_inv(inner_high(tall, tall))
    share = 2 * PANEL // chips
    mine = lax.dynamic_slice_in_dim(inverse, chip * share, share, 0)
    weights = nt(mine, tall)

    width = half // CHUNKS
    out_rows = share // CORES
    outs = []
    for index in range(CHUNKS):
        piece = own[:, :, index * width:(index + 1) * width]
        blocks = [piece] + [shift(piece, "arc", CORES * step) for step in range(1, chips)]
        wide = jnp.concatenate(blocks, 0).reshape(-1, width)
        result = jnp.dot(weights, wide, precision=lax.Precision.HIGH, preferred_element_type=jnp.float32)
        stay = lax.dynamic_slice_in_dim(result, core * out_rows, out_rows, 0)
        leave = lax.dynamic_slice_in_dim(result, (1 - core) * out_rows, out_rows, 0)
        outs.append((stay, swap_core(leave)))
    mine_cols = jnp.concatenate([stay for stay, _ in outs], 1)
    other_cols = jnp.concatenate([moved for _, moved in outs], 1)
    first = core == 0
    return jnp.concatenate([jnp.where(first, mine_cols, other_cols), jnp.where(first, other_cols, mine_cols)], 1)


def inner_high(left, right):
    return lax.dot_general(left, right, (((0,), (0,)), ((), ())), precision=HI, preferred_element_type=jnp.float32)


def solution(mesh):
    return jax.shard_map(
        shards,
        mesh=mesh,
        in_specs=(P("arc", "par"), P("arc", "par"), P()),
        out_specs=P("arc", "par"),
        check_vma=False,
    )
```

```python
import functools

import jax
import jax.numpy as jnp
from jax import lax
from jax.experimental import pallas as pl
from jax.experimental.pallas import tpu as pltpu
from jax.sharding import PartitionSpec as P


PANEL = 256
BLK = 128
CORES = 2
UNITS = 8
RAW_UNITS = (3, 3)
PART_UNITS = (2,)
NB = 64
HI = lax.Precision.HIGHEST
SUB, LANE = 8, 128


def full(row):
    return jnp.broadcast_to(row, (SUB, LANE))


def factor_block(tiles, offset):
    count = len(tiles)
    lanes = lax.broadcasted_iota(jnp.int32, (SUB, LANE), 1)
    subs = lax.broadcasted_iota(jnp.int32, (SUB, LANE), 0)
    tiles = list(tiles)
    for s in range(count):
        base = offset + s * SUB
        cols = {}
        for i in range(s, count):
            for c in range(SUB):
                cols[i, c] = jnp.broadcast_to(tiles[i][:, base + c:base + c + 1], (SUB, LANE))
        a = {(i, j): full(cols[s, j][i:i + 1, :]) for i in range(SUB) for j in range(i + 1)}
        in_diag = (lanes >= base) & (lanes < base + SUB)
        own = jnp.where(in_diag, jnp.where(lanes == base + subs, 1.0, 0.0), tiles[s])
        rows = [full(own[c:c + 1, :]) for c in range(SUB)]
        for j in range(SUB):
            inv = lax.rsqrt(a[j, j])
            low = {i: a[i, j] * inv for i in range(j + 1, SUB)}
            for i in range(j + 1, SUB):
                for m in range(j + 1, i + 1):
                    a[i, m] = a[i, m] - low[i] * low[m]
            rows[j] = rows[j] * inv
            for c in range(j + 1, SUB):
                rows[c] = rows[c] - low[c] * rows[j]
            for i in range(s + 1, count):
                cols[i, j] = cols[i, j] * inv
                for c in range(j + 1, SUB):
                    cols[i, c] = cols[i, c] - low[c] * cols[i, j]
        merged = rows[0]
        for c in range(1, SUB):
            merged = jnp.where(subs == c, rows[c], merged)
        tiles[s] = merged
        for i in range(s + 1, count):
            step = cols[i, 0] * rows[0]
            for c in range(1, SUB):
                step = step + cols[i, c] * rows[c]
            tiles[i] = jnp.where(in_diag, 0.0, tiles[i]) - step
    return tiles


def nt(a, b):
    return lax.dot_general(a, b, (((1,), (1,)), ((), ())), precision=HI, preferred_element_type=jnp.float32)


def nn(a, b):
    return jnp.dot(a, b, precision=HI, preferred_element_type=jnp.float32)


def invert_factor(nb, gram, x_ref, beside=()):
    n = x_ref.shape[0]
    for j in range(0, n, LANE):
        x_ref[j:n, j:j + LANE] = gram[j:n, j:j + LANE]
        if j:
            x_ref[0:j, j:j + LANE] = jnp.zeros((j, LANE), jnp.float32)
    for k in range(n // nb):
        lo, hi = k * nb, (k + 1) * nb
        lane0 = lo // LANE * LANE
        off = lo - lane0
        tiles = [x_ref[lo + SUB * i:lo + SUB * (i + 1), lane0:lane0 + LANE] for i in range(nb // SUB)]
        block = jnp.concatenate(factor_block(tiles, off), 0)
        for task in beside[k::n // nb]:
            task()
        rows = lax.broadcasted_iota(jnp.int32, (nb, LANE), 0)
        lanes = lax.broadcasted_iota(jnp.int32, (nb, LANE), 1)
        inv_rows = jnp.where(lanes <= rows + off, block, 0.0)
        t_wide = jnp.where(lanes >= off, inv_rows, 0.0)
        if lane0:
            x_ref[lo:hi, 0:lane0] = nn(t_wide[:, off:off + nb], x_ref[lo:hi, 0:lane0])
        x_ref[lo:hi, lane0:lane0 + LANE] = inv_rows
        if hi < n:
            rest = x_ref[hi:n, lane0:lane0 + LANE]
            low = nt(rest, t_wide)
            rest_lanes = lax.broadcasted_iota(jnp.int32, (n - hi, LANE), 1)
            x_ref[hi:n, lane0:lane0 + LANE] = jnp.where((rest_lanes >= off) & (rest_lanes < off + nb), 0.0, rest)
            x_ref[hi:n, 0:lane0 + LANE] -= nn(low, x_ref[lo:hi, 0:lane0 + LANE])
            for c in range(hi // LANE * LANE, n, LANE):
                c0 = max(c, hi)
                x_ref[c0:n, c0:c + LANE] -= nt(low[c0 - hi:], low[c0 - hi:c + LANE - hi])


def turned_panel(near_ref, far_ref, t_ref):
    rows = near_ref.shape[0] * near_ref.shape[2]
    for chip in range(near_ref.shape[1]):
        for side, ref in enumerate((near_ref, far_ref)):
            at = (chip * CORES + side) * rows
            t_ref[:, at:at + rows] = ref[:, chip].reshape(rows, PANEL).T


def split(value):
    high = value.astype(jnp.bfloat16)
    return high, (value - high.astype(jnp.float32)).astype(jnp.bfloat16)


def three(left, right, dims):
    (left_high, left_low), (right_high, right_low) = left, right
    total = None
    for a, b in ((left_high, right_high), (left_high, right_low), (left_low, right_high)):
        term = lax.dot_general(a, b, (dims, ((), ())), preferred_element_type=jnp.float32)
        total = term if total is None else total + term
    return total


def first_kernel(near_ref, far_ref, w_ref, t_ref, x_ref):
    turned_panel(near_ref, far_ref, t_ref)
    panel = split(t_ref[...])
    invert_factor(NB, nt(t_ref[...], t_ref[...]), x_ref)
    w_ref[...] = three(split(x_ref[...]), panel, ((1,), (0,)))


def cut_kernel(near_ref, far_ref, w_ref, cut_ref):
    turned_panel(near_ref, far_ref, cut_ref)
    weights = split(w_ref[...])
    mixed = three(weights, split(cut_ref[...]), ((1,), (1,)))
    cut_ref[...] -= three(split(mixed.T), weights, ((1,), (0,)))


def second_kernel(counts, late_ref, cut_ref, w_ref, *refs):
    spans = len(counts)
    blocks, refs = refs[:sum(counts)], refs[sum(counts):]
    x_ref, z_refs = refs[0], refs[1:1 + spans]
    high_ref, low_ref, *buffers = refs[1 + spans:-1]
    sems = refs[-1]
    copies = []
    taken = 0
    for span, count in enumerate(counts):
        at = 0
        for ref in blocks[taken:taken + count]:
            copies.append(pltpu.make_async_copy(ref, buffers[span].at[pl.ds(at, ref.shape[0])], sems.at[len(copies)]))
            copies[-1].start()
            at += ref.shape[0]
        taken += count
    gram = nt(cut_ref[...], cut_ref[...])
    high_ref[...], low_ref[...] = split(jnp.where(late_ref[0] != 0, cut_ref[...], w_ref[...]))
    for copy in copies:
        copy.wait()

    def product(span, at, width):
        depth = buffers[span].shape[0]
        high, low = split(buffers[span][:, at:at + width])
        total = jnp.dot(high_ref[:, :depth], high, preferred_element_type=jnp.float32)
        total += jnp.dot(high_ref[:, :depth], low, preferred_element_type=jnp.float32)
        total += jnp.dot(low_ref[:, :depth], high, preferred_element_type=jnp.float32)
        z_refs[span][:, at:at + width] = total

    tasks = []
    for span in range(spans):
        size = buffers[span].shape[1]
        tasks += [functools.partial(product, span, at, 2 * BLK) for at in range(0, size, 2 * BLK)]
    invert_factor(NB, gram, x_ref, tasks)


def in_vmem(kernel, outs, scratch, flops):
    shapes = [jax.ShapeDtypeStruct(shape, jnp.float32) for shape in outs]
    spec = pl.BlockSpec(memory_space=pltpu.VMEM)

    def call(*args):
        return pl.pallas_call(
            kernel,
            out_shape=shapes,
            in_specs=[spec] * len(args),
            out_specs=[spec] * len(outs),
            scratch_shapes=[pltpu.VMEM(shape, jnp.float32) for shape in scratch],
            cost_estimate=pl.CostEstimate(flops=flops, bytes_accessed=4 * sum(a.size for a in args), transcendentals=0),
        )(*args)

    return call


def eliminate_first(near, far):
    rows = near.size // PANEL * CORES
    flops = 4 * PANEL * PANEL * rows
    return in_vmem(first_kernel, [(PANEL, rows)], [(PANEL, rows), (PANEL, PANEL)], flops)(near, far)[0]


def cut_second(near, far, weights):
    return in_vmem(cut_kernel, [weights.shape], [], 4 * PANEL * weights.size)(near, far, weights)[0]


def eliminate_second(late, cut, weights, spans):
    blocks = [block for span in spans for block in span]
    sizes = [(sum(block.shape[0] for block in span), span[0].shape[1]) for span in spans]
    vmem = pl.BlockSpec(memory_space=pltpu.VMEM)
    work = sum(depth * size for depth, size in sizes)
    return pl.pallas_call(
        functools.partial(second_kernel, [len(span) for span in spans]),
        out_shape=[jax.ShapeDtypeStruct((PANEL, PANEL), jnp.float32)]
        + [jax.ShapeDtypeStruct((PANEL, size), jnp.float32) for _, size in sizes],
        in_specs=[pl.BlockSpec(memory_space=pltpu.SMEM), vmem, vmem] + [pl.BlockSpec(memory_space=pl.ANY)] * len(blocks),
        out_specs=[vmem] * (1 + len(sizes)),
        scratch_shapes=[pltpu.VMEM(cut.shape, jnp.bfloat16)] * 2
        + [pltpu.VMEM(size, jnp.float32) for size in sizes]
        + [pltpu.SemaphoreType.DMA((len(blocks),))],
        cost_estimate=pl.CostEstimate(flops=6 * PANEL * work, bytes_accessed=4 * work, transcendentals=PANEL),
        name="eliminate_second",
    )(late, cut, weights, *blocks)


def shift(array, axis, step):
    size = lax.axis_size(axis)
    return lax.ppermute(array, axis, [(i, (i + step) % size) for i in range(size)])


def swap_core(array):
    return lax.ppermute(array, "arc", [(i, i ^ 1) for i in range(lax.axis_size("arc"))])


def cut_out_kernel(last_panel, local_panels, scale, owner_ref, here_ref, mask_ref, obs_ref, *refs):
    outs, own_ref, turn_ref, (free_ref, last_ref, sems) = refs[:4], refs[4], refs[5], refs[6:]
    free = jnp.where(owner_ref[0] == last_panel, owner_ref[1], owner_ref[0])
    local = lax.rem(free, local_panels)
    bit = lax.rem(here_ref[0], 2)
    per = PANEL // BLK
    targets = ((local * per, free_ref), ((local_panels - 1) * per, last_ref), (here_ref[1], own_ref))
    copies = []
    for index, (place, ref) in enumerate(targets):
        cols = pl.ds(pl.multiple_of(place * BLK, BLK), ref.shape[1])
        copies.append(pltpu.make_async_copy(obs_ref.at[:, cols], ref, sems.at[index]))
        copies[-1].start()
    differ = lax.bitwise_xor(lax.div(free, local_panels), here_ref[0])
    for at in range(turn_ref.shape[0] - 1):
        moved = lax.bitwise_and(lax.shift_right_logical(differ, at), 1)
        turn_ref[at] = jnp.full(turn_ref.shape[1:], moved, jnp.int32)
    last_first = (owner_ref[0] == last_panel).astype(jnp.int32)
    turn_ref[turn_ref.shape[0] - 1] = jnp.full(turn_ref.shape[1:], last_first, jnp.int32)
    for index, (place, ref) in enumerate(targets):
        copies[index].wait()
        for row in range(mask_ref.shape[0]):
            for col in range(ref.shape[1] // BLK):
                mark = mask_ref[row, place + col].astype(jnp.float32) * scale
                spot = (slice(row * BLK, (row + 1) * BLK), slice(col * BLK, (col + 1) * BLK))
                ref[spot] = ref[spot] * mark
        if index == 2:
            break
        for low, out in ((1 - bit, outs[2 * index]), (bit, outs[2 * index + 1])):
            part = out.shape[1]
            for at in range(out.shape[0]):
                out[at] = ref[pl.ds(pl.multiple_of((2 * at + low) * part, part), part), :]


def cut_out(owner, here, mask, obs, own_size, count, last_panel, local_panels, scale):
    rows = obs.shape[0]
    shape = jax.ShapeDtypeStruct((count // 2, rows // count, PANEL), jnp.float32)
    return pl.pallas_call(
        functools.partial(cut_out_kernel, last_panel, local_panels, scale),
        out_shape=[shape] * 4
        + [jax.ShapeDtypeStruct((rows, own_size), jnp.float32)]
        + [jax.ShapeDtypeStruct((count.bit_length(), 1, PANEL), jnp.int32)],
        in_specs=[pl.BlockSpec(memory_space=pltpu.SMEM)] * 3 + [pl.BlockSpec(memory_space=pl.ANY)],
        out_specs=[pl.BlockSpec(memory_space=pltpu.VMEM)] * 6,
        scratch_shapes=[pltpu.VMEM((rows, PANEL), jnp.float32)] * 2 + [pltpu.SemaphoreType.DMA((3,))],
        cost_estimate=pl.CostEstimate(flops=shape.size * 8, bytes_accessed=shape.size * 32, transcendentals=0),
        name="cut_out",
    )(owner, here, mask, obs)


def fan_kernel(*refs):
    crossed, outs = refs[:-2], refs[-2:]
    for panel, out in enumerate(outs):
        for to in range(out.shape[0]):
            for chip, ref in enumerate(crossed):
                out[to, chip] = ref[panel]


def fan(crossed, count):
    shape = jax.ShapeDtypeStruct((count, len(crossed), *crossed[0].shape[1:]), jnp.float32)
    spec = pl.BlockSpec(memory_space=pltpu.VMEM)
    return pl.pallas_call(
        fan_kernel,
        out_shape=[shape, shape],
        in_specs=[spec] * len(crossed),
        out_specs=[spec, spec],
        cost_estimate=pl.CostEstimate(flops=0, bytes_accessed=shape.size * 8, transcendentals=0),
        name="fan",
    )(*crossed)


def scatter(send, keep, moved, pairs_of):
    count, here = lax.axis_size("par"), lax.axis_index("par")
    bit = 1
    while True:
        got = lax.ppermute(send, "par", pairs_of(bit))
        held = jnp.where(moved(bit) != 0, got, keep)
        bit *= 2
        if bit == count:
            return held[0]
        halves = held.reshape(-1, 2, *held.shape[1:])
        low = (here // bit) % 2
        send = lax.dynamic_index_in_dim(halves, 1 - low, 1, keepdims=False)
        keep = lax.dynamic_index_in_dim(halves, low, 1, keepdims=False)


def body(observations, arc_mask, panel_owner):
    row_count, col_count = observations.shape
    arcs, pars = lax.axis_size("arc"), lax.axis_size("par")
    chips = arcs // CORES
    core = lax.axis_index("arc") % CORES
    chip = lax.axis_index("arc") // CORES
    scale = 1.0 / (row_count * arcs) ** 0.5
    local_panels = col_count // PANEL
    last_panel = pars * local_panels - 1
    row_blocks = arc_mask.shape[0]

    half = col_count // CORES

    def half_of(which):
        marks = lax.dynamic_slice_in_dim(arc_mask, which * (half // BLK), half // BLK, 1)
        factors = lax.optimization_barrier(jnp.repeat(marks.astype(jnp.float32) * scale, BLK, axis=1))

        def window(start, size):
            cols = lax.dynamic_slice_in_dim(observations, which * half + start, size, 1)
            return (cols.reshape(row_blocks, BLK, size) * factors[:, None, start:start + size]).reshape(row_count, size)

        return window

    own_window, pair_window = half_of(core), half_of(1 - core)

    def edges(sizes):
        starts = [0]
        for size in sizes:
            starts.append(starts[-1] + size)
        return list(zip(starts, sizes))

    unit = half // UNITS
    parts = [units * unit for units in PART_UNITS] if chips == 2 else []
    raws = [units * unit for units in RAW_UNITS] if chips == 2 else [half // 2, half // 2]
    spans = edges(raws + parts)

    here = jnp.stack([lax.axis_index("par"), core * (half // BLK)])
    *pieces, own, turn = cut_out(panel_owner, here, arc_mask, observations, raws[0], pars, last_panel, local_panels, scale)
    own = [own] + [own_window(start, size) for start, size in spans[1:]]
    free_mine = scatter(
        *pieces[:2], lambda bit: turn[bit.bit_length() - 1], lambda bit: [(i, i ^ bit) for i in range(pars)]
    )
    last_mine = scatter(
        *pieces[2:4],
        lambda bit: (lax.axis_index("par") ^ (pars - 1)) & bit,
        lambda bit: [(i, i ^ bit) for i in range(pars) if i // bit == (pars - 1) // bit],
    )
    last_first = turn[-1] != 0
    both = jnp.stack([jnp.where(last_first, last_mine, free_mine), jnp.where(last_first, free_mine, last_mine)], 0)
    crossed = [both] + [shift(both, "arc", CORES * step) for step in range(1, chips)]
    fan_first, fan_second = fan(crossed, pars)
    near_first = lax.all_to_all(fan_first, "par", 0, 0)
    near_second = lax.all_to_all(fan_second, "par", 0, 0)
    far_first = swap_core(near_first)
    far_second = swap_core(near_second)
    weights_first = eliminate_first(near_first, far_first)
    cut = cut_second(near_second, far_second, weights_first)
    pair = []
    for start, size in spans:
        pair.append(swap_core(pair_window(start, size)))

    def dot_high(left, right):
        return jnp.dot(left, right, precision=lax.Precision.HIGH, preferred_element_type=jnp.float32)

    others = range(1, chips)
    near_rows = 2 * row_count
    results = []
    own_sent, pair_sent = [], []
    for index in range(len(raws)):
        own_sent.append([shift(own[index], "arc", CORES * step) for step in others])
        pair_sent.append([shift(pair[index], "arc", CORES * step) for step in others])
    sums = []
    if parts:
        give = jnp.where(chip == 0, cut[:, :near_rows], weights_first[:, :near_rows])
        for index in range(len(parts)):
            at = len(raws) + index
            sums.append(shift(dot_high(give, jnp.concatenate([own[at], pair[at]], 0)), "arc", CORES))
    blocks = [[own[index], pair[index]] for index in range(len(spans))]
    for index in range(len(raws)):
        for step in range(chips - 1):
            blocks[index] += [own_sent[index][step], pair_sent[index][step]]

    share = 2 * PANEL // chips
    out_rows = share // CORES
    late = (chip * share >= PANEL).astype(jnp.int32).reshape(1)
    inverse_second, *products = eliminate_second(late, cut, weights_first, blocks)
    finish = jnp.concatenate([jnp.eye(PANEL, dtype=jnp.float32), inverse_second], 0)
    mine = lax.dynamic_slice_in_dim(finish, chip * share + core * out_rows, out_rows, 0)
    others = lax.dynamic_slice_in_dim(finish, chip * share + (1 - core) * out_rows, out_rows, 0)
    finish = jnp.concatenate([mine, others], 0)
    for index in range(len(parts)):
        products[len(raws) + index] += sums[index]
    results = [dot_high(finish, product) for product in products]
    outs = [(result[:out_rows], swap_core(result[out_rows:])) for result in results]
    mine_cols = jnp.concatenate([stay for stay, _ in outs], 1)
    other_cols = jnp.concatenate([moved for _, moved in outs], 1)
    first = core == 0
    return jnp.concatenate([jnp.where(first, mine_cols, other_cols), jnp.where(first, other_cols, mine_cols)], 1)


def solution(mesh):
    return jax.shard_map(
        body,
        mesh=mesh,
        in_specs=(P("arc", "par"), P("arc", "par"), P()),
        out_specs=P("arc", "par"),
        check_vma=False,
    )
```
